32 devices in a mesh: dp: 8 (over z, x), tensor: 4 (over y, core).
Axes of the slice: x: 2, y: 2, z: 4, core: 2. Of those that a mesh axis runs over, the one named last changes fastest.
Arguments:
- tokens: bfloat16 [3072, 1024], P('dp'), may hold values from -6 to 6
- segment_ids: int32 [8, 384], P('dp'), may hold values from 0 to 5, never falling along the last dimension, each value on 1 to 192 neighbouring positions
- cotangent: bfloat16 [3072, 1024], P('dp'), may hold values from -6 to 6
- norm1_gain: float32 [1024], replicated, may hold values from 0.5 to 1.5
- norm1_shift: float32 [1024], replicated, may hold values from -3 to 3
- w_qkv: bfloat16 [1024, 3072], P(None, 'tensor'), may hold values from -0.1875 to 0.1875
- b_qkv: float32 [3072], P('tensor'), may hold values from -9 to 9
- w_dense: bfloat16 [1024, 1024], P('tensor'), may hold values from -0.75 to 0.75
- b_dense: float32 [1024], replicated, may hold values from -3 to 3
- norm2_gain: float32 [1024], replicated, may hold values from 0.5 to 1.5
- norm2_shift: float32 [1024], replicated, may hold values from -3 to 3
- w_up: bfloat16 [1024, 4096], P(None, 'tensor'), may hold values from -0.1875 to 0.1875
- b_up: float32 [4096], P('tensor'), may hold values from -3 to 3
- w_down: bfloat16 [4096, 1024], P('tensor'), may hold values from -0.09375 to 0.09375
- b_down: float32 [1024], replicated, may hold values from -3 to 3
Outputs:
- output: bfloat16 [3072, 1024], P('dp')
- grad_input: float32 [3072, 1024], P('dp')
- grad_norm1_gain: float32 [1024], P('dp')
- grad_norm1_shift: float32 [1024], P('dp')
- grad_w_qkv: float32 [1024, 3072], P('dp', 'tensor')
- grad_b_qkv: float32 [3072], P(('tensor', 'dp'))
- grad_w_dense: float32 [1024, 1024], P('tensor', 'dp')
- grad_b_dense: float32 [1024], P('dp')
- grad_norm2_gain: float32 [1024], P('dp')
- grad_norm2_shift: float32 [1024], P('dp')
- grad_w_up: float32 [1024, 4096], P('dp', 'tensor')
- grad_b_up: float32 [4096], P(('tensor', 'dp'))
- grad_w_down: float32 [4096, 1024], P('tensor', 'dp')
- grad_b_down: float32 [1024], P('dp')
The draws below stay inside these ranges and needn't reach their ends.
Inputs may be any that keep to these rules, and one draw needn't show every extreme that they name: `segment_ids`: in each row, ids never fall; each of the 6 sequences has 1 to 192 tokens and one has exactly 192.
All inputs are finite; a program needn't handle non-finite values.
Results may differ from the reference program's by a relative error of at most 0.019.
The reference program's roundings to bfloat16 on the way count: a program that leaves them out, or rounds other values in their place, can miss the bound.
Values sent between devices are 32-bit elements; how exact they have to be, the bound alone decides.
A program may use at most 128 MiB of HBM per device.

```python
import math
import jax
import jax.numpy as jnp
import numpy as np
from jax import lax

D = 1024
H = 16
HD = 64
FF = 4096
TOK_DEV = 384
SEQS = 6
SEG_MAX = 192
TOKENS = 3072
N_DP = 8


def draw_b_qkv(key, part):
    drawn_key, sign_key, spread_key, offset_key = jax.random.split(key, 4)
    drawn_part = jnp.clip(0.5 * jax.random.normal(drawn_key, (H, 3, HD), jnp.float32), -1.5, 1.5)
    levels = jnp.array([0.0, 120.0, 0.0, 260.0], jnp.float32)
    spread = jax.random.uniform(spread_key, (H, HD), jnp.float32, 0.8, 1.2)
    offset = jax.random.randint(offset_key, (), 0, 4)
    strength = jnp.take(levels, (jnp.arange(H) + offset) % 4)
    signs = jnp.where(jax.random.bernoulli(sign_key, 0.5, (H, HD)), 1.0, -1.0)
    aligned = signs * spread * jnp.sqrt(strength / 8.0)[:, None]
    zeros_part = jnp.zeros((H, HD), jnp.float32)
    boost = jnp.stack([aligned, aligned, zeros_part], axis=1)
    return (drawn_part + boost).reshape(3 * D).astype(jnp.float32)


def spiked(values, rng, source, target, blocks, factor):
    def block_of(position):
        return (jnp.arange(values.shape[position]) // (values.shape[position] // blocks)).reshape((-1,) + (1,) * (values.ndim - 1 - position))

    first = jax.random.permutation(rng, blocks)[block_of(target)]
    other_side = (block_of(target) + blocks // 2) % blocks
    return jnp.where((block_of(source) == first) | (block_of(source) == other_side), factor * values, values)


def steps_of(rng, extent, cuts, smallest, largest):
    level = 1.0
    for dim, parts in cuts:
        draws = jax.random.uniform(jax.random.fold_in(jax.random.fold_in(rng, 6), dim), (parts,), jnp.float32, smallest / len(cuts), largest / len(cuts))
        level = level * jnp.repeat(jnp.exp(draws), extent[dim] // parts).reshape((-1,) + (1,) * (len(extent) - 1 - dim))
    return level


def profile(count, total, limit, slope):
    portions = [(1 << 20) // math.isqrt(grade ** slope) + 1 for grade in range(2, count + 1)]
    surplus, given = total - limit - (count - 1), [1] * (count - 1)
    while surplus > 0:
        candidates = [i for i in range(count - 1) if given[i] < limit]
        whole, remaining = sum([portions[i] for i in candidates]), surplus
        for i in candidates:
            more = min(limit - given[i], max(1, remaining * portions[i] // whole), surplus)
            given[i] = given[i] + more
            surplus = surplus - more
    return np.array([limit] + given)


def ragged(own_key, count, total, bound, slope):
    if count == 2:
        one = jax.random.randint(own_key, (), max(1, total - bound), min(bound, total - 1) + 1)
        return jnp.stack([one, total - one])
    sizes = jnp.asarray(profile(count, total, bound, slope), jnp.int32)
    pairs = (count - 1) // 2
    giver, sink = sizes[1:1 + 2 * pairs:2], sizes[2:2 + 2 * pairs:2]
    slack = jnp.minimum(giver - 1, bound - sink)
    shifted = jax.random.randint(jax.random.fold_in(own_key, 1), (pairs,), 0, 1 << 20) % (slack + 1)
    sizes = sizes.at[1:1 + 2 * pairs:2].set(giver - shifted).at[2:2 + 2 * pairs:2].set(sink + shifted)
    return sizes[jax.random.permutation(jax.random.fold_in(own_key, 2), count)]


def gaussian(rng, extent, scale, most, cuts=(), kind=jnp.bfloat16):
    level = steps_of(rng, extent, cuts, -0.22, 0.18) if cuts else 1.0
    values = jax.random.normal(rng, extent, jnp.float32) * scale * level
    return jnp.minimum(jnp.maximum(values, -most), most).astype(kind)


def noise_with(rng, shape, scale, bound, cuts, heavy, held_as=jnp.bfloat16):
    values = scale * jax.random.normal(rng, shape, jnp.float32)
    if cuts:
        values = values * steps_of(rng, shape, cuts, -0.22, 0.18)
    return jnp.clip(spiked(values, jax.random.fold_in(rng, 3), *heavy), -bound, bound).astype(held_as)


def setup_inputs(seed: int = 0) -> dict:
    streams_of = jax.random.split(jax.random.key(seed), 16)
    return {
        "tokens": noise_with(streams_of[0], (TOKENS, D), 1.0, 6.0, ((0, 8),), (0, 1, 8, 2.0)),
        "segment_ids": jax.vmap(lambda own: jnp.searchsorted(jnp.cumsum(ragged(own, SEQS, TOK_DEV, SEG_MAX, 2)), jnp.arange(TOK_DEV), side="right"))(jax.random.split(streams_of[1], N_DP)).reshape((N_DP, TOK_DEV)).astype(jnp.int32),
        "cotangent": noise_with(streams_of[2], (TOKENS, D), 1.0, 6.0, ((0, 8),), (0, 1, 8, 2.0)),
        "norm1_gain": jnp.clip(jax.random.uniform(streams_of[3], (D,), jnp.float32, 0.5, 1.5), 0.5, 1.5),
        "norm1_shift": gaussian(streams_of[4], (D,), 0.5, 3.0, (), jnp.float32),
        "w_qkv": gaussian(streams_of[5], (D, 3 * D), D ** -0.5, 0.1875, ((1, 4),)),
        "b_qkv": draw_b_qkv(jax.random.fold_in(streams_of[15], 71), 0),
        "w_dense": gaussian(streams_of[7], (D, D), HD ** -0.5, 0.75, ((0, 4),)),
        "b_dense": gaussian(streams_of[8], (D,), 0.5, 3.0, (), jnp.float32),
        "norm2_gain": jnp.clip(jax.random.uniform(streams_of[9], (D,), jnp.float32, 0.5, 1.5), 0.5, 1.5),
        "norm2_shift": gaussian(streams_of[10], (D,), 0.5, 3.0, (), jnp.float32),
        "w_up": gaussian(streams_of[11], (D, FF), D ** -0.5, 0.1875, ((1, 4),)),
        "b_up": gaussian(streams_of[12], (FF,), 0.5, 3.0, ((0, 4),), jnp.float32),
        "w_down": gaussian(streams_of[13], (FF, D), FF ** -0.5, 0.09375, ((0, 4),)),
        "b_down": gaussian(streams_of[14], (D,), 0.5, 3.0, (), jnp.float32),
    }


EPSILON = 1e-05
GELU_COEF = math.sqrt(2.0 / math.pi)

def layer_norm(values, gain, shift):
    average = lax.optimization_barrier(jnp.mean(values, axis=-1, keepdims=True))
    centered = values - average
    variance = lax.optimization_barrier(jnp.mean(centered * centered, axis=-1, keepdims=True))
    inverse = lax.rsqrt(variance + EPSILON)
    normed = centered * inverse
    return (normed * gain + shift, normed, inverse)

def norm_backward(upstream, normed, inverse, gain):
    scaled = upstream * gain
    return inverse * (scaled - lax.optimization_barrier(jnp.mean(scaled, axis=-1, keepdims=True)) - normed * lax.optimization_barrier(jnp.mean(scaled * normed, axis=-1, keepdims=True)))

def gelu_pair(inputs):
    tangent = jnp.tanh(GELU_COEF * (inputs + 0.044715 * inputs * inputs * inputs))
    result = 0.5 * inputs * (1.0 + tangent)
    derivative = 0.5 * (1.0 + tangent) + 0.5 * inputs * (1.0 - tangent * tangent) * GELU_COEF * (1.0 + 3.0 * 0.044715 * inputs * inputs)
    return (result, derivative)

def shard_pass(tokens, segments, cotangent, norm1_gain, norm1_shift, w_qkv, b_qkv, w_dense, b_dense, norm2_gain, norm2_shift, w_up, b_up, w_down, b_down):
    row_count = tokens.shape[0]
    scaling = 1.0 / math.sqrt(HD)
    inputs = tokens.astype(jnp.float32)
    first_out, normed1, inverse1 = layer_norm(inputs, norm1_gain, norm1_shift)
    first_in = first_out.astype(jnp.bfloat16)
    joined = (jnp.dot(first_in, w_qkv, preferred_element_type=jnp.float32) + b_qkv).astype(jnp.bfloat16)
    joined = joined.reshape(row_count, H, 3, HD)
    queries = joined[:, :, 0].astype(jnp.float32)
    key_vecs = joined[:, :, 1].astype(jnp.float32)
    val_vecs = joined[:, :, 2].astype(jnp.float32)
    slopes = 2.0 ** (-8.0 * (jnp.arange(H) + 1).astype(jnp.float32) / H)
    places = jnp.arange(row_count)
    offset = (places[None, :] - places[:, None]).astype(jnp.float32)
    allowed = (segments[:, None] == segments[None, :]) & (places[None, :] <= places[:, None])
    raw_scores = jnp.einsum('ihe,jhe->hij', queries, key_vecs)
    scores = jnp.where(allowed[None], raw_scores * scaling + slopes[:, None, None] * offset[None], -1e+30)
    highest = lax.optimization_barrier(jnp.max(scores, axis=-1, keepdims=True))
    log_total = highest + jnp.log(lax.optimization_barrier(jnp.sum(jnp.exp(scores - highest), axis=-1, keepdims=True)))
    attn_probs = jnp.exp(scores - log_total)
    probs_b = attn_probs.astype(jnp.bfloat16).astype(jnp.float32)
    context = jnp.einsum('hij,jhe->ihe', probs_b, val_vecs).astype(jnp.bfloat16).reshape(row_count, D)
    hidden = inputs + jnp.dot(context, w_dense, preferred_element_type=jnp.float32) + b_dense
    second_out, normed2, inverse2 = layer_norm(hidden, norm2_gain, norm2_shift)
    second_in = second_out.astype(jnp.bfloat16)
    upward = jnp.dot(second_in, w_up, preferred_element_type=jnp.float32) + b_up
    activated, gelu_slope = gelu_pair(upward)
    activated_b = activated.astype(jnp.bfloat16)
    output = (hidden + jnp.dot(activated_b, w_down, preferred_element_type=jnp.float32) + b_down).astype(jnp.bfloat16)
    grad_out = cotangent.astype(jnp.float32)
    grad_w_down = jnp.dot(activated_b.T, cotangent, preferred_element_type=jnp.float32)
    grad_b_down = lax.optimization_barrier(jnp.sum(grad_out, axis=0))
    grad_up = jnp.dot(cotangent, w_down.T, preferred_element_type=jnp.float32) * gelu_slope
    grad_up_b = grad_up.astype(jnp.bfloat16)
    grad_w_up = jnp.dot(second_in.T, grad_up_b, preferred_element_type=jnp.float32)
    grad_b_up = lax.optimization_barrier(jnp.sum(grad_up, axis=0))
    grad_norm2 = jnp.dot(grad_up_b, w_up.T, preferred_element_type=jnp.float32)
    grad_gain2 = lax.optimization_barrier(jnp.sum(grad_norm2 * normed2, axis=0))
    grad_shift2 = lax.optimization_barrier(jnp.sum(grad_norm2, axis=0))
    grad_hidden = grad_out + norm_backward(grad_norm2, normed2, inverse2, norm2_gain)
    grad_hidden_b = grad_hidden.astype(jnp.bfloat16)
    grad_w_dense = jnp.dot(context.T, grad_hidden_b, preferred_element_type=jnp.float32)
    grad_b_dense = lax.optimization_barrier(jnp.sum(grad_hidden, axis=0))
    grad_context = jnp.dot(grad_hidden_b, w_dense.T, preferred_element_type=jnp.float32).astype(jnp.bfloat16)
    grad_context = grad_context.reshape(row_count, H, HD).astype(jnp.float32)
    grad_vals = jnp.einsum('hij,ihe->jhe', probs_b, grad_context)
    grad_probs = jnp.einsum('ihe,jhe->hij', grad_context, val_vecs)
    row_inner = lax.optimization_barrier(jnp.sum(attn_probs * grad_probs, axis=-1, keepdims=True))
    grad_scores = (attn_probs * (grad_probs - row_inner)).astype(jnp.bfloat16).astype(jnp.float32)
    grad_queries = jnp.einsum('hij,jhe->ihe', grad_scores, key_vecs) * scaling
    grad_keys = jnp.einsum('hij,ihe->jhe', grad_scores, queries) * scaling
    grad_joined = jnp.stack([grad_queries, grad_keys, grad_vals], axis=2).reshape(row_count, 3 * D)
    grad_joined_b = grad_joined.astype(jnp.bfloat16)
    grad_w_qkv = jnp.dot(first_in.T, grad_joined_b, preferred_element_type=jnp.float32)
    grad_b_qkv = lax.optimization_barrier(jnp.sum(grad_joined, axis=0))
    grad_norm1 = jnp.dot(grad_joined_b, w_qkv.T, preferred_element_type=jnp.float32)
    grad_gain1 = lax.optimization_barrier(jnp.sum(grad_norm1 * normed1, axis=0))
    grad_shift1 = lax.optimization_barrier(jnp.sum(grad_norm1, axis=0))
    grad_input = grad_hidden + norm_backward(grad_norm1, normed1, inverse1, norm1_gain)
    grads = (grad_gain1, grad_shift1, grad_w_qkv, grad_b_qkv, grad_w_dense, grad_b_dense, grad_gain2, grad_shift2, grad_w_up, grad_b_up, grad_w_down, grad_b_down)
    return (output, grad_input, grads)

def reference(tokens, segment_ids, cotangent, norm1_gain, norm1_shift, w_qkv, b_qkv, w_dense, b_dense, norm2_gain, norm2_shift, w_up, b_up, w_down, b_down):
    shards = segment_ids.shape[0]
    token_blocks = tokens.reshape(shards, TOK_DEV, D)
    cot_blocks = cotangent.reshape(shards, TOK_DEV, D)
    initial = (jnp.zeros((D,), jnp.float32), jnp.zeros((D,), jnp.float32), jnp.zeros((D, 3 * D), jnp.float32), jnp.zeros((3 * D,), jnp.float32), jnp.zeros((D, D), jnp.float32), jnp.zeros((D,), jnp.float32), jnp.zeros((D,), jnp.float32), jnp.zeros((D,), jnp.float32), jnp.zeros((D, FF), jnp.float32), jnp.zeros((FF,), jnp.float32), jnp.zeros((FF, D), jnp.float32), jnp.zeros((D,), jnp.float32))

    def step_fn(carry, pieces):
        block, segments, cot_block = pieces
        output, grad_input, grads = shard_pass(block, segments, cot_block, norm1_gain, norm1_shift, w_qkv, b_qkv, w_dense, b_dense, norm2_gain, norm2_shift, w_up, b_up, w_down, b_down)
        carry = jax.tree.map(lambda left, right: left + right, carry, grads)
        return (carry, (output, grad_input))
    totals, (outputs, grad_inputs) = lax.scan(step_fn, initial, (token_blocks, segment_ids, cot_blocks))
    return (outputs.reshape(shards * TOK_DEV, D), grad_inputs.reshape(shards * TOK_DEV, D)) + tuple(totals)
```

```python
import functools
import math

import jax
import jax.numpy as jnp
from jax import lax
from jax.experimental import pallas as pl
from jax.experimental.pallas import tpu as pltpu
from jax.sharding import PartitionSpec as P

H = 16
HD = 64


EPSILON = 1e-05
GELU_COEF = math.sqrt(2.0 / math.pi)


def layer_norm(values, gain, shift):
    average = jnp.mean(values, axis=-1, keepdims=True)
    centered = values - average
    variance = jnp.mean(centered * centered, axis=-1, keepdims=True)
    inverse = lax.rsqrt(variance + EPSILON)
    normed = centered * inverse
    return (normed * gain + shift, normed, inverse)


def norm_backward(upstream, normed, inverse, gain):
    scaled = upstream * gain
    return inverse * (
        scaled
        - jnp.mean(scaled, axis=-1, keepdims=True)
        - normed * jnp.mean(scaled * normed, axis=-1, keepdims=True)
    )


def gelu_pair(inputs):
    tangent = jnp.tanh(GELU_COEF * (inputs + 0.044715 * inputs * inputs * inputs))
    result = 0.5 * inputs * (1.0 + tangent)
    derivative = 0.5 * (1.0 + tangent) + 0.5 * inputs * (1.0 - tangent * tangent) * GELU_COEF * (
        1.0 + 3.0 * 0.044715 * inputs * inputs
    )
    return (result, derivative)


def head_scores(queries, key_vecs, slopes, offset, allowed, scaling):
    raw_scores = jnp.einsum("ihe,jhe->hij", queries, key_vecs, preferred_element_type=jnp.float32)
    return jnp.where(
        allowed[None], raw_scores * scaling + slopes[:, None, None] * offset[None], -1e30
    )

CHUNKS = 4
LAG = 2
MESH = pl.DeviceIdType.MESH
MIB = 1024 * 1024


def add_rows(dst, terms):
    rows, columns = dst.shape
    step = math.gcd(rows, 32 if columns > 128 else 256)

    def body(i, carry):
        part = pl.ds(pl.multiple_of(i * step, step), step)
        total = terms[0][part, :]
        for term in terms[1:]:
            total = total + term[part, :]
        dst[part, :] = total
        return carry

    lax.fori_loop(0, rows // step, body, 0)


def exchange_kernel(kinds, n_sum, *refs):
    n_red = len(kinds)
    refs = list(refs)

    def take(count):
        taken = refs[:count]
        del refs[:count]
        return taken

    grads, parts = take(n_red), take(n_sum)
    outs, sums = take(n_red), take(n_sum)
    rx, ru, rd = take(n_red), take(n_red), take(n_red)
    if n_red:
        xs, xr, us, ur, ds, dr = take(6)
    if n_sum:
        near, mine, far = take(3)
        cs, cr, ys, yr, bs, br = take(6)
    barrier = pltpu.get_barrier_semaphore()
    expected = 0
    if n_red:
        place = lax.axis_index("dp")
        z, x = place // 2, place % 2
        other_x = {"dp": z * 2 + 1 - x}
        above, below = {"dp": place + 2}, {"dp": place - 2}
        pl.semaphore_signal(barrier, inc=1, device_id=other_x, device_id_type=MESH)
        low, high = z > 0, z < 3

        @pl.when(high)
        def _():
            pl.semaphore_signal(barrier, inc=1, device_id=above, device_id_type=MESH)

        @pl.when(low)
        def _():
            pl.semaphore_signal(barrier, inc=1, device_id=below, device_id_type=MESH)

        expected = expected + 1 + jnp.minimum(z, 1) + jnp.minimum(3 - z, 1)
    if n_sum:
        seat = lax.axis_index("tensor")
        y, core = seat // 2, seat % 2
        other_core = {"tensor": y * 2 + 1 - core}
        other_y = {"tensor": (1 - y) * 2 + core}
        pl.semaphore_signal(barrier, inc=1, device_id=other_core, device_id_type=MESH)
        pl.semaphore_signal(barrier, inc=1, device_id=other_y, device_id_type=MESH)
        expected = expected + 2
    pl.semaphore_wait(barrier, expected)

    def shard(m, target, column):
        ref = grads[m]
        index = 2 * target + column
        if kinds[m] == "rows":
            size = ref.shape[0] // 8
            return ref.at[pl.ds(pl.multiple_of(index * size, size), size), :]
        size = ref.shape[1] // 8
        return ref.at[:, pl.ds(pl.multiple_of(index * size, size), size)]

    def send(src, dst, send_sem, recv_sem, device):
        return pltpu.make_async_remote_copy(
            src_ref=src,
            dst_ref=dst,
            send_sem=send_sem,
            recv_sem=recv_sem,
            device_id=device,
            device_id_type=MESH,
        )

    def across(m, t):
        return send(shard(m, t, 1 - x), rx[m].at[t], xs.at[m, t], xr.at[m, t], other_x)

    def up(m, t):
        return send(rx[m].at[t], ru[m].at[t], us.at[m, t], ur.at[m, t], above)

    def down(m, t):
        return send(rx[m].at[t], rd[m].at[t], ds.at[m, t], dr.at[m, t], below)

    def near_copy(a, k):
        half = parts[a].shape[0] // 2
        size = half // CHUNKS
        start = pl.multiple_of((1 - core) * half + k * size, 8)
        return send(
            parts[a].at[pl.ds(start, size), :],
            near.at[a, k],
            cs.at[a, k],
            cr.at[a, k],
            other_core,
        )

    def far_copy(a, k):
        return send(mine.at[a, k], far.at[a, k], ys.at[a, k], yr.at[a, k], other_y)

    def own(a, k):
        half = parts[a].shape[0] // 2
        size = half // CHUNKS
        return pl.ds(pl.multiple_of(core * half + k * size, 8), size)

    def back_copy(a, k):
        rows = own(a, k)
        return send(
            sums[a].at[rows, :], sums[a].at[rows, :], bs.at[a, k], br.at[a, k], other_core
        )

    for a in range(n_sum):
        for k in range(CHUNKS):
            near_copy(a, k).start()
    order = [(m, t) for m in range(n_red) for t in (3, 0, 2, 1)]
    for m, t in order:
        across(m, t).start()

    def open_sum(a, k):
        near_copy(a, k).wait_recv()
        add_rows(mine.at[a, k], [parts[a].at[own(a, k), :], near.at[a, k]])
        far_copy(a, k).start()

    def close_sum(a, k):
        far_copy(a, k).wait_recv()
        add_rows(sums[a].at[own(a, k), :], [mine.at[a, k], far.at[a, k]])
        back_copy(a, k).start()

    def first_hop(m, t):
        across(m, t).wait_recv()
        add_rows(rx[m].at[t], [shard(m, t, x), rx[m].at[t]])
        if t > 0:

            @pl.when(z == 0)
            def _():
                up(m, t).start()

        if t < 3:

            @pl.when(z == 3)
            def _():
                down(m, t).start()

    def next_hop(m, t):
        @pl.when((z > 0) & (z < t))
        def _():
            up(m, t).wait_recv()
            add_rows(rx[m].at[t], [rx[m].at[t], ru[m].at[t]])
            up(m, t).start()

        @pl.when((z < 3) & (z > t))
        def _():
            down(m, t).wait_recv()
            add_rows(rx[m].at[t], [rx[m].at[t], rd[m].at[t]])
            down(m, t).start()

    def last_hop(m, t):
        @pl.when(z == t)
        def _():
            terms = [rx[m].at[t]]
            if t > 0:
                up(m, t).wait_recv()
                terms.append(ru[m].at[t])
            if t < 3:
                down(m, t).wait_recv()
                terms.append(rd[m].at[t])
            add_rows(outs[m], terms)

    for a in range(n_sum):
        for k in range(CHUNKS):
            open_sum(a, k)
    closing = [(a, k) for a in range(n_sum) for k in range(CHUNKS)]
    for n in range(len(order) + LAG):
        if n > 0 or not order:
            for _ in range(CHUNKS):
                if closing:
                    close_sum(*closing.pop(0))
        if n < len(order):
            first_hop(*order[n])
        if n >= LAG and order:
            next_hop(*order[n - LAG])
    while closing:
        close_sum(*closing.pop(0))
    for m, t in order:
        last_hop(m, t)
    for a in range(n_sum):
        for k in range(CHUNKS):
            back_copy(a, k).wait_recv()
            near_copy(a, k).wait_send()
            far_copy(a, k).wait_send()
            back_copy(a, k).wait_send()
    for m, t in order:
        across(m, t).wait_send()

        @pl.when(z < t)
        def _():
            up(m, t).wait_send()

        @pl.when(z > t)
        def _():
            down(m, t).wait_send()


def exchange(grads, kinds, parts, collective_id):
    n_red, n_sum = len(grads), len(parts)
    f32 = jnp.float32
    shapes = []
    for grad, kind in zip(grads, kinds):
        rows, columns = grad.shape
        shapes.append((rows // 8, columns) if kind == "rows" else (rows, columns // 8))
    out_shape = [jax.ShapeDtypeStruct(s, f32) for s in shapes]
    out_shape += [jax.ShapeDtypeStruct(p.shape, f32) for p in parts]
    scratch = []
    if n_red:
        for _ in range(3):
            scratch += [pltpu.VMEM((4,) + s, f32) for s in shapes]
        scratch += [pltpu.SemaphoreType.DMA((n_red, 4))] * 6
    if n_sum:
        rows, columns = parts[0].shape
        scratch += [pltpu.VMEM((n_sum, CHUNKS, rows // 2 // CHUNKS, columns), f32)] * 3
        scratch += [pltpu.SemaphoreType.DMA((n_sum, CHUNKS))] * 6
    vmem = pl.BlockSpec(memory_space=pltpu.VMEM)
    return pl.pallas_call(
        functools.partial(exchange_kernel, tuple(kinds), n_sum),
        out_shape=out_shape,
        in_specs=[vmem] * (n_red + n_sum),
        out_specs=[vmem] * (n_red + n_sum),
        scratch_shapes=scratch,
        compiler_params=pltpu.CompilerParams(
            collective_id=collective_id, has_side_effects=True, vmem_limit_bytes=56 * MIB
        ),
    )(*grads, *parts)


def paired(size_tensor):
    return size_tensor == 4


def sum_parts(parts, size_tensor, collective_id):
    if paired(size_tensor):
        return exchange([], [], parts, collective_id)
    return [lax.psum(part, "tensor") for part in parts]


def scatter(grads, kinds, parts, sizes, collective_id):
    if sizes == (8, 4):
        done = exchange(grads, kinds, parts, collective_id)
        return done[: len(grads)], done[len(grads) :]
    reduced = [
        lax.psum_scatter(g, "dp", scatter_dimension=0 if k == "rows" else 1, tiled=True)
        for g, k in zip(grads, kinds)
    ]
    return reduced, (sum_parts(parts, sizes[1], collective_id) if parts else [])


def scatter_vectors(vectors, sizes, collective_id):
    n_dp = sizes[0]
    widths = [v.shape[0] // n_dp for v in vectors]
    widest = -(-max(widths) // 128) * 128
    table = jnp.stack(
        [jnp.pad(v.reshape(n_dp, -1), ((0, 0), (0, widest - w))) for v, w in zip(vectors, widths)],
        axis=1,
    ).reshape(n_dp * len(vectors), widest)
    (mine,), _ = scatter([table], ["rows"], [], sizes, collective_id)
    return [mine[i, :w] for i, w in enumerate(widths)]


def local(
    sizes,
    tokens,
    segment_ids,
    cotangent,
    norm1_gain,
    norm1_shift,
    w_qkv,
    b_qkv,
    w_dense,
    b_dense,
    norm2_gain,
    norm2_shift,
    w_up,
    b_up,
    w_down,
    b_down,
):
    segments = segment_ids[0]
    row_count = tokens.shape[0]
    heads_here = w_qkv.shape[1] // (3 * HD)
    head_start = lax.axis_index("tensor") * heads_here
    scaling = 1.0 / math.sqrt(HD)
    slopes = 2.0 ** (-8.0 * (head_start + jnp.arange(heads_here) + 1).astype(jnp.float32) / H)
    places = jnp.arange(row_count)
    offset = (places[None, :] - places[:, None]).astype(jnp.float32)
    allowed = (segments[:, None] == segments[None, :]) & (places[None, :] <= places[:, None])
    inputs = tokens.astype(jnp.float32)
    first_out, normed1, inverse1 = layer_norm(inputs, norm1_gain, norm1_shift)
    first_in = first_out.astype(jnp.bfloat16)
    joined = (jnp.dot(first_in, w_qkv, preferred_element_type=jnp.float32) + b_qkv).astype(
        jnp.bfloat16
    )
    joined = joined.reshape(row_count, heads_here, 3, HD)
    queries = joined[:, :, 0]
    key_vecs = joined[:, :, 1]
    val_vecs = joined[:, :, 2]
    scores = head_scores(queries, key_vecs, slopes, offset, allowed, scaling)
    highest = jnp.max(scores, axis=-1, keepdims=True)
    log_total = highest + jnp.log(jnp.sum(jnp.exp(scores - highest), axis=-1, keepdims=True))
    probs_b = jnp.exp(scores - log_total).astype(jnp.bfloat16)
    context = jnp.einsum(
        "hij,jhe->ihe", probs_b, val_vecs, preferred_element_type=jnp.float32
    ).astype(jnp.bfloat16)
    context = context.reshape(row_count, heads_here * HD)
    (attended,) = sum_parts(
        [jnp.dot(context, w_dense, preferred_element_type=jnp.float32)], sizes[1], 0
    )
    hidden = inputs + attended + b_dense
    second_out, normed2, inverse2 = layer_norm(hidden, norm2_gain, norm2_shift)
    second_in = second_out.astype(jnp.bfloat16)
    upward = jnp.dot(second_in, w_up, preferred_element_type=jnp.float32) + b_up
    activated, gelu_slope = gelu_pair(upward)
    activated_b = activated.astype(jnp.bfloat16)
    mixed = jnp.dot(activated_b, w_down, preferred_element_type=jnp.float32)
    grad_out = cotangent.astype(jnp.float32)
    grad_w_down = jnp.dot(activated_b.T, cotangent, preferred_element_type=jnp.float32)
    grad_b_down = jnp.sum(grad_out, axis=0)
    grad_up = jnp.dot(cotangent, w_down.T, preferred_element_type=jnp.float32) * gelu_slope
    grad_up_b = grad_up.astype(jnp.bfloat16)
    grad_w_up = jnp.dot(second_in.T, grad_up_b, preferred_element_type=jnp.float32)
    grad_b_up = jnp.sum(grad_up, axis=0)
    grad_norm2 = jnp.dot(grad_up_b, w_up.T, preferred_element_type=jnp.float32)
    (grad_w_up, grad_w_down), (grad_norm2, mixed) = scatter(
        [grad_w_up, grad_w_down], ["rows", "columns"], [grad_norm2, mixed], sizes, 1
    )
    output = (hidden + mixed + b_down).astype(jnp.bfloat16)
    grad_gain2 = jnp.sum(grad_norm2 * normed2, axis=0)
    grad_shift2 = jnp.sum(grad_norm2, axis=0)
    grad_hidden = grad_out + norm_backward(grad_norm2, normed2, inverse2, norm2_gain)
    grad_hidden_b = grad_hidden.astype(jnp.bfloat16)
    grad_w_dense = jnp.dot(context.T, grad_hidden_b, preferred_element_type=jnp.float32)
    grad_b_dense = jnp.sum(grad_hidden, axis=0)
    grad_context = jnp.dot(grad_hidden_b, w_dense.T, preferred_element_type=jnp.float32).astype(
        jnp.bfloat16
    )
    grad_context = grad_context.reshape(row_count, heads_here, HD)
    scores_again = head_scores(queries, key_vecs, slopes, offset, allowed, scaling)
    probs_again = jnp.exp(scores_again - log_total)
    probs_again_b = probs_again.astype(jnp.bfloat16)
    grad_vals = jnp.einsum(
        "hij,ihe->jhe", probs_again_b, grad_context, preferred_element_type=jnp.float32
    )
    grad_probs = jnp.einsum(
        "ihe,jhe->hij", grad_context, val_vecs, preferred_element_type=jnp.float32
    )
    row_inner = jnp.sum(probs_again * grad_probs, axis=-1, keepdims=True)
    grad_scores = (probs_again * (grad_probs - row_inner)).astype(jnp.bfloat16)
    grad_queries = (
        jnp.einsum("hij,jhe->ihe", grad_scores, key_vecs, preferred_element_type=jnp.float32)
        * scaling
    )
    grad_keys = (
        jnp.einsum("hij,ihe->jhe", grad_scores, queries, preferred_element_type=jnp.float32)
        * scaling
    )
    grad_joined = jnp.stack([grad_queries, grad_keys, grad_vals], axis=2).reshape(
        row_count, 3 * heads_here * HD
    )
    grad_joined_b = grad_joined.astype(jnp.bfloat16)
    grad_w_qkv = jnp.dot(first_in.T, grad_joined_b, preferred_element_type=jnp.float32)
    grad_b_qkv = jnp.sum(grad_joined, axis=0)
    grad_norm1 = jnp.dot(grad_joined_b, w_qkv.T, preferred_element_type=jnp.float32)
    (grad_w_qkv, grad_w_dense), (grad_norm1,) = scatter(
        [grad_w_qkv, grad_w_dense], ["rows", "columns"], [grad_norm1], sizes, 2
    )
    grad_gain1 = jnp.sum(grad_norm1 * normed1, axis=0)
    grad_shift1 = jnp.sum(grad_norm1, axis=0)
    grad_input = grad_hidden + norm_backward(grad_norm1, normed1, inverse1, norm1_gain)
    vectors = scatter_vectors(
        [
            grad_gain1,
            grad_shift1,
            grad_b_qkv,
            grad_b_dense,
            grad_gain2,
            grad_shift2,
            grad_b_up,
            grad_b_down,
        ],
        sizes,
        3,
    )
    gain1, shift1, b_qkv_part, b_dense_part, gain2, shift2, b_up_part, b_down_part = vectors
    return (
        output,
        grad_input,
        gain1,
        shift1,
        grad_w_qkv,
        b_qkv_part,
        grad_w_dense,
        b_dense_part,
        gain2,
        shift2,
        grad_w_up,
        b_up_part,
        grad_w_down,
        b_down_part,
    )


def solution(mesh):
    in_specs = (
        P("dp", None),
        P("dp", None),
        P("dp", None),
        P(),
        P(),
        P(None, "tensor"),
        P("tensor"),
        P("tensor", None),
        P(),
        P(),
        P(),
        P(None, "tensor"),
        P("tensor"),
        P("tensor", None),
        P(),
    )
    out_specs = (
        P("dp", None),
        P("dp", None),
        P("dp"),
        P("dp"),
        P("dp", "tensor"),
        P(("tensor", "dp")),
        P("tensor", "dp"),
        P("dp"),
        P("dp"),
        P("dp"),
        P("dp", "tensor"),
        P(("tensor", "dp")),
        P("tensor", "dp"),
        P("dp"),
    )
    sizes = (mesh.shape["dp"], mesh.shape["tensor"])
    body = functools.partial(local, sizes)
    return jax.shard_map(body, mesh=mesh, in_specs=in_specs, out_specs=out_specs, check_vma=False)
```

```python
import functools
import math

import jax
import jax.numpy as jnp
from jax import lax
from jax.experimental import pallas as pl
from jax.experimental.pallas import tpu as pltpu
from jax.sharding import PartitionSpec as P

H = 16
HD = 64


EPSILON = 1e-05
GELU_COEF = math.sqrt(2.0 / math.pi)


def layer_norm(values, gain, shift):
    average = jnp.mean(values, axis=-1, keepdims=True)
    centered = values - average
    variance = jnp.mean(centered * centered, axis=-1, keepdims=True)
    inverse = lax.rsqrt(variance + EPSILON)
    normed = centered * inverse
    return (normed * gain + shift, normed, inverse)


def norm_backward(upstream, normed, inverse, gain):
    scaled = upstream * gain
    return inverse * (
        scaled
        - jnp.mean(scaled, axis=-1, keepdims=True)
        - normed * jnp.mean(scaled * normed, axis=-1, keepdims=True)
    )


def gelu_pair(inputs):
    tangent = jnp.tanh(GELU_COEF * (inputs + 0.044715 * inputs * inputs * inputs))
    result = 0.5 * inputs * (1.0 + tangent)
    derivative = 0.5 * (1.0 + tangent) + 0.5 * inputs * (1.0 - tangent * tangent) * GELU_COEF * (
        1.0 + 3.0 * 0.044715 * inputs * inputs
    )
    return (result, derivative)


def head_scores(queries, key_vecs, slopes, offset, allowed, scaling):
    raw_scores = jnp.einsum("ihe,jhe->hij", queries, key_vecs, preferred_element_type=jnp.float32)
    return jnp.where(
        allowed[None], raw_scores * scaling + slopes[:, None, None] * offset[None], -1e30
    )

CHUNKS = 4
PIECES = 2
LAG = 2
MESH = pl.DeviceIdType.MESH
MIB = 1024 * 1024


def add_rows(dst, terms):
    rows, columns = dst.shape
    step = math.gcd(rows, 32 if columns > 128 else 256)

    def body(i, carry):
        part = pl.ds(pl.multiple_of(i * step, step), step)
        total = terms[0][part, :]
        for term in terms[1:]:
            total = total + term[part, :]
        dst[part, :] = total
        return carry

    lax.fori_loop(0, rows // step, body, 0)


def exchange_kernel(kinds, n_sum, n_late, n_extra, middle, *refs):
    n_red = len(kinds)
    refs = list(refs)

    def take(count):
        taken = refs[:count]
        del refs[:count]
        return taken

    late_sum = 1 if middle else 0
    grads, parts = take(n_red - n_late), take(n_sum - late_sum)
    extra = take(n_extra)
    outs, sums = take(n_red), take(n_sum)
    more = take(2) if middle else []
    rx, ru, rd = take(n_red), take(n_red), take(n_red)
    if n_red:
        xs, xr, us, ur, ds, dr = take(6)
    if n_sum:
        near, mine, far = take(3)
        cs, cr, ys, yr, bs, br = take(6)
    if middle:
        grads += take(n_late)
        parts += take(1)
    barrier = pltpu.get_barrier_semaphore()
    expected = 0
    if n_red:
        place = lax.axis_index("dp")
        z, x = place // 2, place % 2
        other_x = {"dp": z * 2 + 1 - x}
        above, below = {"dp": place + 2}, {"dp": place - 2}
        pl.semaphore_signal(barrier, inc=1, device_id=other_x, device_id_type=MESH)
        low, high = z > 0, z < 3

        @pl.when(high)
        def _():
            pl.semaphore_signal(barrier, inc=1, device_id=above, device_id_type=MESH)

        @pl.when(low)
        def _():
            pl.semaphore_signal(barrier, inc=1, device_id=below, device_id_type=MESH)

        expected = expected + 1 + jnp.minimum(z, 1) + jnp.minimum(3 - z, 1)
    if n_sum:
        seat = lax.axis_index("tensor")
        y, core = seat // 2, seat % 2
        other_core = {"tensor": y * 2 + 1 - core}
        other_y = {"tensor": (1 - y) * 2 + core}
        pl.semaphore_signal(barrier, inc=1, device_id=other_core, device_id_type=MESH)
        pl.semaphore_signal(barrier, inc=1, device_id=other_y, device_id_type=MESH)
        expected = expected + 2
    pl.semaphore_wait(barrier, expected)

    def shard(m, target, column, p):
        ref = grads[m]
        index = 2 * target + column
        if kinds[m] == "rows":
            size = ref.shape[0] // 8
            piece = size // pieces(m)
            start = pl.multiple_of(index * size + p * piece, piece)
            return ref.at[pl.ds(start, piece), :]
        size = ref.shape[1] // 8
        piece = ref.shape[0] // pieces(m)
        start = pl.multiple_of(index * size, size)
        return ref.at[pl.ds(p * piece, piece), pl.ds(start, size)]

    def pieces(m):
        return PIECES if outs[m].shape[0] % (8 * PIECES) == 0 else 1

    def slot(ref, m, t, p):
        piece = outs[m].shape[0] // pieces(m)
        return ref[m].at[t, pl.ds(p * piece, piece), :]

    def send(src, dst, send_sem, recv_sem, device):
        return pltpu.make_async_remote_copy(
            src_ref=src,
            dst_ref=dst,
            send_sem=send_sem,
            recv_sem=recv_sem,
            device_id=device,
            device_id_type=MESH,
        )

    def across(m, t, p):
        return send(
            shard(m, t, 1 - x, p), slot(rx, m, t, p), xs.at[m, t, p], xr.at[m, t, p], other_x
        )

    def up(m, t, p):
        return send(
            slot(rx, m, t, p), slot(ru, m, t, p), us.at[m, t, p], ur.at[m, t, p], above
        )

    def down(m, t, p, last=False):
        dst = slot(rd, m, 0, p) if last else slot(ru, m, t, p)
        return send(slot(rx, m, t, p), dst, ds.at[m, t, p], dr.at[m, t, p], below)

    def near_copy(a, k):
        half = parts[a].shape[0] // 2
        size = half // CHUNKS
        start = pl.multiple_of((1 - core) * half + k * size, 8)
        return send(
            parts[a].at[pl.ds(start, size), :],
            near.at[a, k],
            cs.at[a, k],
            cr.at[a, k],
            other_core,
        )

    def far_copy(a, k):
        return send(mine.at[a, k], far.at[a, k], ys.at[a, k], yr.at[a, k], other_y)

    def own(a, k):
        half = parts[a].shape[0] // 2
        size = half // CHUNKS
        return pl.ds(pl.multiple_of(core * half + k * size, 8), size)

    def back_copy(a, k):
        rows = own(a, k)
        return send(
            sums[a].at[rows, :], sums[a].at[rows, :], bs.at[a, k], br.at[a, k], other_core
        )

    def pieces_of(ms):
        return [(m, t, p) for m in ms for t in (3, 0, 2, 1) for p in range(pieces(m))]

    def start_sum(a):
        for k in range(CHUNKS):
            near_copy(a, k).start()

    def start_across(m):
        for piece in pieces_of([m]):
            across(*piece).start()

    for a in range(n_sum - late_sum):
        start_sum(a)
    for m in range(n_red - n_late):
        start_across(m)
    order = pieces_of(range(n_red))

    def open_sum(a, k):
        near_copy(a, k).wait_recv()
        add_rows(mine.at[a, k], [parts[a].at[own(a, k), :], near.at[a, k]])
        far_copy(a, k).start()

    def close_sum(a, k):
        far_copy(a, k).wait_recv()
        add_rows(sums[a].at[own(a, k), :], [mine.at[a, k], far.at[a, k]])
        back_copy(a, k).start()

    def first_hop(m, t, p):
        across(m, t, p).wait_recv()
        add_rows(slot(rx, m, t, p), [shard(m, t, x, p), slot(rx, m, t, p)])
        if t > 0:

            @pl.when(z == 0)
            def _():
                up(m, t, p).start()

        if t < 3:

            @pl.when(z == 3)
            def _():
                down(m, t, p, t == 2).start()

    def next_hop(m, t, p):
        @pl.when((z > 0) & (z < t))
        def _():
            up(m, t, p).wait_recv()
            add_rows(slot(rx, m, t, p), [slot(rx, m, t, p), slot(ru, m, t, p)])
            up(m, t, p).start()

        for here in (1, 2):
            if here > t:

                @pl.when(z == here)
                def _():
                    down(m, t, p).wait_recv()
                    add_rows(slot(rx, m, t, p), [slot(rx, m, t, p), slot(ru, m, t, p)])
                    down(m, t, p, t == here - 1).start()

    def last_hop(m, t, p):
        @pl.when(z == t)
        def _():
            terms = [slot(rx, m, t, p)]
            if t > 0:
                up(m, t, p).wait_recv()
                terms.append(slot(ru, m, t, p))
            if t < 3:
                down(m, t, p).wait_recv()
                terms.append(slot(rd, m, 0, p))
            piece = outs[m].shape[0] // pieces(m)
            add_rows(outs[m].at[pl.ds(p * piece, piece), :], terms)

    state = {"first": 0, "next": 0}

    def hop():
        n = state["first"]
        if n < len(order):
            first_hop(*order[n])
            state["first"] += 1
        if state["next"] < len(order) and n >= state["next"] + LAG:
            next_hop(*order[state["next"]])
            state["next"] += 1

    early = range(n_sum - late_sum)
    for a in early:
        for k in range(CHUNKS):
            open_sum(a, k)
    if middle:
        hop()
        hop()
    for k in range(CHUNKS):
        if n_sum:
            close_sum(0, k)
    if middle:
        for k in range(CHUNKS):
            back_copy(0, k).wait_recv()
        steps = middle(sums[0], extra, more, grads[n_red - n_late :], parts[-1], refs)
        closing = [(a, k) for a in early if a for k in range(CHUNKS)]
        for step, started in steps:
            step()
            if started is not None:
                start_across(n_red - n_late + started)
            if closing:
                close_sum(*closing.pop(0))
            hop()
        while closing:
            close_sum(*closing.pop(0))
        start_sum(n_sum - 1)
        hop()
        for k in range(CHUNKS):
            open_sum(n_sum - 1, k)
        hop()
        hop()
        hop()
        for k in range(CHUNKS):
            close_sum(n_sum - 1, k)
    else:
        for a in early:
            for k in range(CHUNKS):
                if a:
                    close_sum(a, k)
    while state["next"] < len(order) if n_red else False:
        hop() if state["first"] < len(order) else drain(state, next_hop, order)
    for piece in order:
        last_hop(*piece)
    for a in range(n_sum):
        for k in range(CHUNKS):
            if not (middle and a == 0):
                back_copy(a, k).wait_recv()
            near_copy(a, k).wait_send()
            far_copy(a, k).wait_send()
            back_copy(a, k).wait_send()
    for m, t, p in order:
        across(m, t, p).wait_send()

        @pl.when(z < t)
        def _():
            up(m, t, p).wait_send()

        @pl.when(z > t)
        def _():
            down(m, t, p).wait_send()


def drain(state, next_hop, order):
    next_hop(*order[state["next"]])
    state["next"] += 1


def contract(left, right, left_axis, right_axis):
    return lax.dot_general(
        left, right, (((left_axis,), (right_axis,)), ((), ())), preferred_element_type=jnp.float32
    )


def backward_steps(grad_norm2, extra, more, grads, part, scratch):
    (
        cotangent,
        normed2,
        inverse2,
        gain2,
        context_t,
        w_dense_t,
        probs,
        queries,
        key_vecs,
        val_vecs,
        first_in_t,
        w_qkv_t,
    ) = extra
    grad_hidden, grad_joined = more
    grad_w_dense, grad_w_qkv = grads
    grad_hidden_b, grad_context, thirds, grad_joined_b = scratch
    heads = probs.shape[0]
    rows = cotangent.shape[0]
    scaling = 1.0 / math.sqrt(HD)

    def hidden_step():
        def body(i, carry):
            at = pl.ds(pl.multiple_of(i * 16, 16), 16)
            change = norm_backward(
                grad_norm2[at, :], normed2[at, :], inverse2[at, :], gain2[...]
            )
            value = cotangent[at, :].astype(jnp.float32) + change
            grad_hidden[at, :] = value
            grad_hidden_b[at, :] = value.astype(jnp.bfloat16)
            return carry

        lax.fori_loop(0, rows // 16, body, 0)

    def dense_step():
        def body(i, carry):
            at = pl.ds(pl.multiple_of(i * 64, 64), 64)
            grad_w_dense[at, :] = contract(context_t[at, :], grad_hidden_b[...], 1, 0)
            return carry

        lax.fori_loop(0, context_t.shape[0] // 64, body, 0)

    def context_step():
        def body(i, carry):
            at = pl.ds(pl.multiple_of(i * 128, 128), 128)
            value = contract(grad_hidden_b[at, :], w_dense_t[...], 1, 0).astype(jnp.bfloat16)
            for h in range(heads):
                grad_context[h, at, :] = value[:, h * HD : (h + 1) * HD]
            return carry

        lax.fori_loop(0, rows // 128, body, 0)

    def attention_step():
        def body(h, carry):
            prob = probs[h]
            upstream = grad_context[h]
            grad_probs = contract(upstream, val_vecs[h], 1, 1)
            row_inner = jnp.sum(prob * grad_probs, axis=-1, keepdims=True)
            grad_scores = (prob * (grad_probs - row_inner)).astype(jnp.bfloat16)
            thirds[h, 2] = contract(prob.astype(jnp.bfloat16), upstream, 0, 0)
            thirds[h, 0] = contract(grad_scores, key_vecs[h], 1, 0) * scaling
            thirds[h, 1] = contract(grad_scores, queries[h], 0, 0) * scaling
            return carry

        lax.fori_loop(0, heads, body, 0)

    def joined_step():
        for h in range(heads):
            for third in range(3):
                start = (3 * h + third) * HD
                grad_joined[:, start : start + HD] = thirds[h, third]

        def body(i, carry):
            at = pl.ds(pl.multiple_of(i * 32, 32), 32)
            grad_joined_b[at, :] = grad_joined[at, :].astype(jnp.bfloat16)
            return carry

        lax.fori_loop(0, rows // 32, body, 0)

    def qkv_step():
        def body(i, carry):
            at = pl.ds(pl.multiple_of(i * 128, 128), 128)
            grad_w_qkv[at, :] = contract(first_in_t[at, :], grad_joined_b[...], 1, 0)
            return carry

        lax.fori_loop(0, first_in_t.shape[0] // 128, body, 0)

    def norm_step():
        def body(i, carry):
            at = pl.ds(pl.multiple_of(i * 64, 64), 64)
            part[at, :] = contract(grad_joined_b[at, :], w_qkv_t[...], 1, 0)
            return carry

        lax.fori_loop(0, rows // 64, body, 0)

    return [
        (hidden_step, None),
        (dense_step, 0),
        (context_step, None),
        (attention_step, None),
        (joined_step, None),
        (qkv_step, 1),
        (norm_step, None),
    ]


def exchange(grads, kinds, parts, collective_id, extra=(), middle=None):
    f32 = jnp.float32
    shapes, full, late = [], [g.shape for g in grads], []
    sums = [p.shape for p in parts]
    more = []
    kinds = list(kinds)
    if middle:
        rows, width = extra[0].shape
        columns = extra[4].shape[0]
        late = [(columns, width), (width, 3 * columns)]
        kinds += ["columns", "rows"]
        sums.append((rows, width))
        more = [(rows, width), (rows, 3 * columns)]
    for (rows, columns), kind in zip(full + late, kinds):
        shapes.append((rows // 8, columns) if kind == "rows" else (rows, columns // 8))
    n_red, n_sum = len(shapes), len(sums)
    out_shape = [jax.ShapeDtypeStruct(s, f32) for s in shapes + sums + more]
    scratch = []
    if n_red:
        for slots in (4, 4, 1):
            scratch += [pltpu.VMEM((slots,) + s, f32) for s in shapes]
        scratch += [pltpu.SemaphoreType.DMA((n_red, 4, PIECES))] * 6
    if n_sum:
        rows, columns = sums[0]
        scratch += [pltpu.VMEM((n_sum, CHUNKS, rows // 2 // CHUNKS, columns), f32)] * 3
        scratch += [pltpu.SemaphoreType.DMA((n_sum, CHUNKS))] * 6
    if middle:
        heads, rows, _ = extra[6].shape
        width = extra[0].shape[1]
        scratch += [pltpu.VMEM(s, f32) for s in late] + [pltpu.VMEM(sums[-1], f32)]
        scratch += [
            pltpu.VMEM((rows, width), jnp.bfloat16),
            pltpu.VMEM((heads, rows, HD), jnp.bfloat16),
            pltpu.VMEM((heads, 3, rows, HD), f32),
            pltpu.VMEM((rows, 3 * heads * HD), jnp.bfloat16),
        ]
    vmem = pl.BlockSpec(memory_space=pltpu.VMEM)
    return pl.pallas_call(
        functools.partial(exchange_kernel, tuple(kinds), n_sum, len(late), len(extra), middle),
        out_shape=out_shape,
        in_specs=[vmem] * (len(grads) + len(parts) + len(extra)),
        out_specs=[vmem] * len(out_shape),
        scratch_shapes=scratch,
        compiler_params=pltpu.CompilerParams(
            collective_id=collective_id,
            has_side_effects=True,
            vmem_limit_bytes=(63 if middle else 40) * MIB,
        ),
    )(*grads, *parts, *extra)


def paired(size_tensor):
    return size_tensor == 4


def sum_parts(parts, size_tensor, collective_id):
    if paired(size_tensor):
        return exchange([], [], parts, collective_id)
    return [lax.psum(part, "tensor") for part in parts]


def scatter(grads, kinds, parts, sizes, collective_id):
    if sizes == (8, 4):
        done = exchange(grads, kinds, parts, collective_id)
        return done[: len(grads)], done[len(grads) :]
    reduced = [
        lax.psum_scatter(g, "dp", scatter_dimension=0 if k == "rows" else 1, tiled=True)
        for g, k in zip(grads, kinds)
    ]
    return reduced, (sum_parts(parts, sizes[1], collective_id) if parts else [])


def scatter_vectors(vectors, sizes, collective_id):
    n_dp = sizes[0]
    widths = [v.shape[0] // n_dp for v in vectors]
    widest = -(-max(widths) // 128) * 128
    table = jnp.stack(
        [jnp.pad(v.reshape(n_dp, -1), ((0, 0), (0, widest - w))) for v, w in zip(vectors, widths)],
        axis=1,
    ).reshape(n_dp * len(vectors), widest)
    (mine,), _ = scatter([table], ["rows"], [], sizes, collective_id)
    return [mine[i, :w] for i, w in enumerate(widths)]


def local(
    sizes,
    tokens,
    segment_ids,
    cotangent,
    norm1_gain,
    norm1_shift,
    w_qkv,
    b_qkv,
    w_dense,
    b_dense,
    norm2_gain,
    norm2_shift,
    w_up,
    b_up,
    w_down,
    b_down,
):
    segments = segment_ids[0]
    row_count = tokens.shape[0]
    heads_here = w_qkv.shape[1] // (3 * HD)
    head_start = lax.axis_index("tensor") * heads_here
    scaling = 1.0 / math.sqrt(HD)
    slopes = 2.0 ** (-8.0 * (head_start + jnp.arange(heads_here) + 1).astype(jnp.float32) / H)
    places = jnp.arange(row_count)
    offset = (places[None, :] - places[:, None]).astype(jnp.float32)
    allowed = (segments[:, None] == segments[None, :]) & (places[None, :] <= places[:, None])
    inputs = tokens.astype(jnp.float32)
    first_out, normed1, inverse1 = layer_norm(inputs, norm1_gain, norm1_shift)
    first_in = first_out.astype(jnp.bfloat16)
    joined = (jnp.dot(first_in, w_qkv, preferred_element_type=jnp.float32) + b_qkv).astype(
        jnp.bfloat16
    )
    joined = joined.reshape(row_count, heads_here, 3, HD)
    queries = joined[:, :, 0]
    key_vecs = joined[:, :, 1]
    val_vecs = joined[:, :, 2]
    scores = head_scores(queries, key_vecs, slopes, offset, allowed, scaling)
    highest = jnp.max(scores, axis=-1, keepdims=True)
    log_total = highest + jnp.log(jnp.sum(jnp.exp(scores - highest), axis=-1, keepdims=True))
    probs = jnp.exp(scores - log_total)
    probs_b = probs.astype(jnp.bfloat16)
    context = jnp.einsum(
        "hij,jhe->ihe", probs_b, val_vecs, preferred_element_type=jnp.float32
    ).astype(jnp.bfloat16)
    context = context.reshape(row_count, heads_here * HD)
    (attended,) = sum_parts(
        [jnp.dot(context, w_dense, preferred_element_type=jnp.float32)], sizes[1], 0
    )
    hidden = inputs + attended + b_dense
    second_out, normed2, inverse2 = layer_norm(hidden, norm2_gain, norm2_shift)
    second_in = second_out.astype(jnp.bfloat16)
    upward = jnp.dot(second_in, w_up, preferred_element_type=jnp.float32) + b_up
    activated, gelu_slope = gelu_pair(upward)
    activated_b = activated.astype(jnp.bfloat16)
    mixed = jnp.dot(activated_b, w_down, preferred_element_type=jnp.float32)
    grad_out = cotangent.astype(jnp.float32)
    grad_w_down = jnp.dot(activated_b.T, cotangent, preferred_element_type=jnp.float32)
    grad_b_down = jnp.sum(grad_out, axis=0)
    grad_up = jnp.dot(cotangent, w_down.T, preferred_element_type=jnp.float32) * gelu_slope
    grad_up_b = grad_up.astype(jnp.bfloat16)
    grad_w_up = jnp.dot(second_in.T, grad_up_b, preferred_element_type=jnp.float32)
    grad_b_up = jnp.sum(grad_up, axis=0)
    grad_norm2 = jnp.dot(grad_up_b, w_up.T, preferred_element_type=jnp.float32)
    if sizes == (8, 4):
        extra = (
            cotangent,
            normed2,
            inverse2,
            norm2_gain[None],
            context.T,
            w_dense.T,
            probs,
            queries.transpose(1, 0, 2),
            key_vecs.transpose(1, 0, 2),
            val_vecs.transpose(1, 0, 2),
            first_in.T,
            w_qkv.T,
        )
        (
            grad_w_up,
            grad_w_down,
            grad_w_dense,
            grad_w_qkv,
            grad_norm2,
            mixed,
            grad_norm1,
            grad_hidden,
            grad_joined,
        ) = exchange(
            [grad_w_up, grad_w_down],
            ["rows", "columns"],
            [grad_norm2, mixed],
            1,
            extra,
            backward_steps,
        )
    else:
        (grad_w_up, grad_w_down), (grad_norm2, mixed) = scatter(
            [grad_w_up, grad_w_down], ["rows", "columns"], [grad_norm2, mixed], sizes, 1
        )
        grad_hidden = grad_out + norm_backward(grad_norm2, normed2, inverse2, norm2_gain)
        grad_hidden_b = grad_hidden.astype(jnp.bfloat16)
        grad_w_dense = jnp.dot(context.T, grad_hidden_b, preferred_element_type=jnp.float32)
        grad_context = jnp.dot(grad_hidden_b, w_dense.T, preferred_element_type=jnp.float32).astype(
            jnp.bfloat16
        )
        grad_context = grad_context.reshape(row_count, heads_here, HD)
        scores_again = head_scores(queries, key_vecs, slopes, offset, allowed, scaling)
        probs_again = jnp.exp(scores_again - log_total)
        probs_again_b = probs_again.astype(jnp.bfloat16)
        grad_vals = jnp.einsum(
            "hij,ihe->jhe", probs_again_b, grad_context, preferred_element_type=jnp.float32
        )
        grad_probs = jnp.einsum(
            "ihe,jhe->hij", grad_context, val_vecs, preferred_element_type=jnp.float32
        )
        row_inner = jnp.sum(probs_again * grad_probs, axis=-1, keepdims=True)
        grad_scores = (probs_again * (grad_probs - row_inner)).astype(jnp.bfloat16)
        grad_queries = (
            jnp.einsum("hij,jhe->ihe", grad_scores, key_vecs, preferred_element_type=jnp.float32)
            * scaling
        )
        grad_keys = (
            jnp.einsum("hij,ihe->jhe", grad_scores, queries, preferred_element_type=jnp.float32)
            * scaling
        )
        grad_joined = jnp.stack([grad_queries, grad_keys, grad_vals], axis=2).reshape(
            row_count, 3 * heads_here * HD
        )
        grad_joined_b = grad_joined.astype(jnp.bfloat16)
        grad_w_qkv = jnp.dot(first_in.T, grad_joined_b, preferred_element_type=jnp.float32)
        grad_norm1 = jnp.dot(grad_joined_b, w_qkv.T, preferred_element_type=jnp.float32)
        (grad_w_qkv, grad_w_dense), (grad_norm1,) = scatter(
            [grad_w_qkv, grad_w_dense], ["rows", "columns"], [grad_norm1], sizes, 2
        )
    output = (hidden + mixed + b_down).astype(jnp.bfloat16)
    grad_gain2 = jnp.sum(grad_norm2 * normed2, axis=0)
    grad_shift2 = jnp.sum(grad_norm2, axis=0)
    grad_b_dense = jnp.sum(grad_hidden, axis=0)
    grad_b_qkv = jnp.sum(grad_joined, axis=0)
    grad_gain1 = jnp.sum(grad_norm1 * normed1, axis=0)
    grad_shift1 = jnp.sum(grad_norm1, axis=0)
    grad_input = grad_hidden + norm_backward(grad_norm1, normed1, inverse1, norm1_gain)
    vectors = scatter_vectors(
        [
            grad_gain1,
            grad_shift1,
            grad_b_qkv,
            grad_b_dense,
            grad_gain2,
            grad_shift2,
            grad_b_up,
            grad_b_down,
        ],
        sizes,
        3,
    )
    gain1, shift1, b_qkv_part, b_dense_part, gain2, shift2, b_up_part, b_down_part = vectors
    return (
        output,
        grad_input,
        gain1,
        shift1,
        grad_w_qkv,
        b_qkv_part,
        grad_w_dense,
        b_dense_part,
        gain2,
        shift2,
        grad_w_up,
        b_up_part,
        grad_w_down,
        b_down_part,
    )


def solution(mesh):
    in_specs = (
        P("dp", None),
        P("dp", None),
        P("dp", None),
        P(),
        P(),
        P(None, "tensor"),
        P("tensor"),
        P("tensor", None),
        P(),
        P(),
        P(),
        P(None, "tensor"),
        P("tensor"),
        P("tensor", None),
        P(),
    )
    out_specs = (
        P("dp", None),
        P("dp", None),
        P("dp"),
        P("dp"),
        P("dp", "tensor"),
        P(("tensor", "dp")),
        P("tensor", "dp"),
        P("dp"),
        P("dp"),
        P("dp"),
        P("dp", "tensor"),
        P(("tensor", "dp")),
        P("tensor", "dp"),
        P("dp"),
    )
    sizes = (mesh.shape["dp"], mesh.shape["tensor"])
    body = functools.partial(local, sizes)
    return jax.shard_map(body, mesh=mesh, in_specs=in_specs, out_specs=out_specs, check_vma=False)
```
